256 devices in a mesh: lat: 4 (over z_lo), wave: 64 (over z_hi, y, x, core).
Axes of the slice: x: 4, y: 4, z: 8 (z_hi: 2, z_lo: 4; z = z_hi * 4 + z_lo), core: 2. Of those that a mesh axis runs over, the one named last changes fastest.
Arguments:
- fourier: bfloat16 [2, 1024, 1024, 128], P(None, ('lat', 'wave')), may hold values from -6 to 6
- cycle_points: int32 [1024], P(('lat', 'wave')), may hold values from 20 to 4120, as said below
- wave_table: int32 [1024], replicated, may hold values from 0 to 1023, as said below
- legendre: bfloat16 [1024, 1024, 1024], P('wave', 'lat'), as said below
Outputs:
- spectral: bfloat16 [1024, 1024, 128], P('wave', 'lat')
The draws below stay inside these ranges and needn't reach their ends.
Inputs may be any that keep to these rules, and one draw needn't show every extreme that they name: wave_table is a permutation of 0 to 1023; slots 16 q to 16 q + 15 hold 16 consecutive wavenumbers in rising order. legendre[r, k, l] is zero wherever the degree wave_table[r] + 2 j + p exceeds 1024 - 1, with p = 1 if l >= 512 else 0 and j = l - p * 512. `cycle_points`: cycle k has about 4 k + 20 points.
All inputs are finite; a program needn't handle non-finite values.
Results may differ from the reference program's by a relative error of at most 0.0085.
Values may be sent and summed in bfloat16 or wider, within the bound.
No kernel may reach another device: no remote copies, remote signals or barrier semaphores. Data moves between devices by JAX's collectives and lax.ppermute only.
A program may use at most 128 MiB of HBM per device.

```python
import jax
import jax.numpy as jnp
from jax import lax

M = 1024
NH = 1024
C = 128
N_LAT = 4


def order_helper(key):
    sub = jax.random.fold_in(key, 7)
    groups = jax.random.permutation(sub, M // 16).astype(jnp.int32)
    return (groups[:, None] * 16 + jnp.arange(16, dtype=jnp.int32)[None, :]).reshape(M)


def draw_wave_table(key, part):
    return order_helper(key)


def draw_cycle_points(key, part):
    cycles = jnp.arange(NH, dtype=jnp.int32)
    jitter = jax.random.randint(jax.random.fold_in(key, 3), (NH,), 1, 4).astype(jnp.int32)
    jitter = jitter.at[0].set(1).at[NH - 1].set(3)
    return 16 + 4 * cycles + 4 * jitter


def draw_legendre(key, part):
    table = order_helper(key)
    sub = jax.random.fold_in(key, 11)
    values = jax.random.normal(sub, (M, NH, M), jnp.float32)
    values = values * NH ** (-0.5)
    columns = jnp.arange(M, dtype=jnp.int32)
    parity = (columns >= M // 2).astype(jnp.int32)
    degree_step = columns - parity * (M // 2)
    limit = (M - 1 - table[:, None] - parity[None, :]) // 2
    valid = (degree_step[None, :] <= limit).astype(jnp.float32)
    return (values * valid[:, None, :]).astype(jnp.bfloat16)


def shard_levels(own_key, dims, pieces, smallest, high):
    gain = 1.0
    for axis_at, shards_of in pieces:
        draws = jax.random.uniform(jax.random.fold_in(jax.random.fold_in(own_key, 6), axis_at), (shards_of,), jnp.float32, smallest / len(pieces), high / len(pieces))
        gain = gain * jnp.repeat(jnp.exp(draws), dims[axis_at] // shards_of).reshape((-1,) + (1,) * (len(dims) - 1 - axis_at))
    return gain


def scatter_about(stream_key, extent, width, most, cuts=(), held_as=jnp.bfloat16):
    level = shard_levels(stream_key, extent, cuts, -0.22, 0.18) if cuts else 1.0
    drawn = jax.random.normal(stream_key, extent, jnp.float32) * width * level
    return jnp.minimum(jnp.maximum(drawn, -most), most).astype(held_as)


def setup_inputs(seed: int = 0) -> dict:
    seeds = jax.random.split(jax.random.key(seed), 5)
    return {
        "fourier": scatter_about(seeds[0], (2, NH, M, C), 1.0, 6.0, ((1, 256),)),
        "cycle_points": draw_cycle_points(jax.random.fold_in(seeds[4], 71), 0),
        "wave_table": draw_wave_table(jax.random.fold_in(seeds[4], 71), 0),
        "legendre": draw_legendre(jax.random.fold_in(seeds[4], 71), 0),
    }


def band_sums(columns, inputs):
    cycle_band = NH // N_LAT
    left = columns.astype(jnp.float32).reshape(N_LAT, cycle_band, columns.shape[1])
    right = inputs.astype(jnp.float32).reshape(N_LAT, cycle_band, inputs.shape[1])
    parts = jnp.einsum("bkl,bkc->blc", left, right).astype(jnp.bfloat16)
    return jnp.sum(parts.astype(jnp.float32), axis=0)


def reference(fourier, cycle_points, wave_table, legendre):
    waves = jnp.arange(M, dtype=jnp.int32)
    present = (2 * waves[None, :] < cycle_points[:, None]).astype(jnp.bfloat16)
    kept = fourier * present[None, :, :, None]
    north = kept[0].astype(jnp.float32)
    south = kept[1].astype(jnp.float32)
    even_part = (north + south).astype(jnp.bfloat16)
    odd_part = (north - south).astype(jnp.bfloat16)
    half = M // 2

    def one_slot(pair):
        column_set, wave = pair
        even_in = lax.dynamic_index_in_dim(even_part, wave, 1, keepdims=False)
        odd_in = lax.dynamic_index_in_dim(odd_part, wave, 1, keepdims=False)
        first = band_sums(column_set[:, :half], even_in)
        second = band_sums(column_set[:, half:], odd_in)
        return jnp.concatenate([first, second], axis=0).astype(jnp.bfloat16)

    return lax.map(one_slot, (legendre, wave_table.astype(jnp.int32)))
```

```python
import functools

import jax
import jax.numpy as jnp
from jax import lax
from jax.experimental import pallas as pl
from jax.experimental.pallas import tpu as pltpu
from jax.sharding import PartitionSpec as P


def parts_kernel(groups, width, points_ref, table_ref, fourier_ref, out_ref):
    cycles = fourier_ref.shape[1]
    channels = fourier_ref.shape[3]

    @pl.loop(0, groups)
    def _(q):
        first = pl.multiple_of(table_ref[q * width] // width * width, width)
        for k in range(cycles):
            wave = first + lax.broadcasted_iota(jnp.int32, (width, channels), 0)
            keep = 2 * wave < points_ref[k]
            north = fourier_ref[0, k, pl.ds(first, width), :].astype(jnp.float32)
            south = fourier_ref[1, k, pl.ds(first, width), :].astype(jnp.float32)
            out_ref[q, 0, k] = jnp.where(keep, north + south, 0.0).astype(out_ref.dtype)
            out_ref[q, 1, k] = jnp.where(keep, north - south, 0.0).astype(out_ref.dtype)


def make_parts(fourier, cycle_points, wave_table, groups):
    _, cycles, waves, channels = fourier.shape
    width = waves // groups
    return pl.pallas_call(
        functools.partial(parts_kernel, groups, width),
        out_shape=jax.ShapeDtypeStruct((groups, 2, cycles, width, channels), fourier.dtype),
        in_specs=[
            pl.BlockSpec(memory_space=pltpu.SMEM),
            pl.BlockSpec(memory_space=pltpu.SMEM),
            pl.BlockSpec(memory_space=pltpu.VMEM),
        ],
        out_specs=pl.BlockSpec(memory_space=pltpu.VMEM),
        name="make_parts",
    )(cycle_points, wave_table, fourier)


def band_kernel(parts_ref, legendre_ref, out_ref):
    blocks, _, _, cols = out_ref.shape
    half = blocks // 2
    for b in range(blocks):
        part = parts_ref[b // half, 0]
        piece = legendre_ref[0, :, b * cols : (b + 1) * cols]
        total = lax.dot_general(part, piece, (((0,), (0,)), ((), ())), preferred_element_type=jnp.float32)
        out_ref[b, 0] = total.astype(out_ref.dtype)


def band_sums(parts, legendre, blocks):
    _, slots, cycles, channels = parts.shape
    columns = legendre.shape[2]
    cols = columns // blocks
    return pl.pallas_call(
        band_kernel,
        grid=(slots,),
        out_shape=jax.ShapeDtypeStruct((blocks, slots, channels, cols), parts.dtype),
        in_specs=[
            pl.BlockSpec((2, 1, cycles, channels), lambda m: (0, m, 0, 0)),
            pl.BlockSpec((1, cycles, columns), lambda m: (m, 0, 0)),
        ],
        out_specs=pl.BlockSpec((blocks, 1, channels, cols), lambda m: (0, m, 0, 0)),
        name="band_sums",
    )(parts, legendre)


def per_device(fourier, cycle_points, wave_table, legendre):
    groups = lax.axis_size("wave")
    bands = lax.axis_size("lat")
    sent = make_parts(fourier, cycle_points, wave_table, groups)
    got = lax.all_to_all(sent, "wave", split_axis=0, concat_axis=0, tiled=True)
    _, _, cycles, width, channels = got.shape
    parts = jnp.transpose(got, (1, 3, 0, 2, 4)).reshape(2, width, groups * cycles, channels)
    sums = band_sums(parts, legendre, bands)
    moved = lax.all_to_all(sums, "lat", split_axis=0, concat_axis=0, tiled=True)
    total = jnp.sum(moved.astype(jnp.float32), axis=0).astype(jnp.bfloat16)
    return jnp.transpose(total, (0, 2, 1))


def solution(mesh):
    placed = (P(None, ("lat", "wave"), None, None), P(("lat", "wave")), P(), P("wave", "lat", None))
    return jax.shard_map(
        per_device, mesh=mesh, in_specs=placed, out_specs=P("wave", "lat", None), check_vma=False
    )
```

```python
import functools

import jax
import jax.numpy as jnp
from jax import lax
from jax.experimental import pallas as pl
from jax.experimental.pallas import tpu as pltpu
from jax.sharding import PartitionSpec as P

CHUNKS = (4,4,4,4)
FINISH_BYTES = 8000000
LATE = True


def parts_kernel(groups, width, points_ref, table_ref, fourier_ref, out_ref):
    cycles = fourier_ref.shape[1]
    channels = fourier_ref.shape[3]
    row = lax.broadcasted_iota(jnp.int32, (width, channels), 0)

    @pl.loop(0, groups, unroll=2)
    def _(q):
        first = pl.multiple_of(table_ref[q * width] // width * width, width)
        rows = pl.ds(first, width)
        for k in range(cycles):
            keep = row < (points_ref[k] + 1) // 2 - first
            north = fourier_ref[0, k, rows, :].astype(jnp.float32)
            south = fourier_ref[1, k, rows, :].astype(jnp.float32)
            out_ref[q, 0, k] = jnp.where(keep, north + south, 0.0).astype(out_ref.dtype)
            out_ref[q, 1, k] = jnp.where(keep, north - south, 0.0).astype(out_ref.dtype)


def make_parts(fourier, cycle_points, wave_table, groups):
    _, cycles, waves, channels = fourier.shape
    width = waves // groups
    return pl.pallas_call(
        functools.partial(parts_kernel, groups, width),
        out_shape=jax.ShapeDtypeStruct((groups, 2, cycles, width, channels), fourier.dtype),
        in_specs=[
            pl.BlockSpec(memory_space=pltpu.SMEM),
            pl.BlockSpec(memory_space=pltpu.SMEM),
            pl.BlockSpec(memory_space=pltpu.VMEM),
        ],
        out_specs=pl.BlockSpec(memory_space=pltpu.VMEM),
        name="make_parts",
    )(cycle_points, wave_table, fourier)


def band_kernel(me_ref, parts_ref, legendre_ref, *refs):
    mine_ref, near_ref, far_ref, cross_ref = refs[-4:]
    me = me_ref[0]
    cols = mine_ref.shape[1]
    for slot in range(mine_ref.shape[0]):
        for flip, ref in ((3, cross_ref), (2, far_ref), (0, mine_ref), (1, near_ref)):
            shard = me ^ flip
            piece = legendre_ref[slot, :, pl.ds(pl.multiple_of(shard * cols, cols), cols)]
            total = lax.dot_general(
                piece, parts_ref[shard // 2, slot], (((0,), (0,)), ((), ())), preferred_element_type=jnp.float32
            )
            ref[slot] = total.astype(ref.dtype)


def band_sums(me, parts, legendre, first, whole):
    _, slots, cycles, channels = parts.shape
    columns = legendre.shape[2]
    cols = columns // 4
    step = 2 if slots % 2 == 0 else 1
    skip = first // step
    every = jax.ShapeDtypeStruct((legendre.shape[0], cols, channels), parts.dtype)
    chunk = jax.ShapeDtypeStruct((slots, cols, channels), parts.dtype)
    every_spec = pl.BlockSpec((step, cols, channels), lambda m, w: (skip + m, 0, 0))
    chunk_spec = pl.BlockSpec((step, cols, channels), lambda m, w: (m, 0, 0))
    return pl.pallas_call(
        band_kernel,
        grid_spec=pltpu.PrefetchScalarGridSpec(
            num_scalar_prefetch=1,
            grid=(slots // step,),
            in_specs=[
                pl.BlockSpec((2, step, cycles, channels), lambda m, w: (0, m, 0, 0)),
                pl.BlockSpec((step, cycles, columns), lambda m, w: (skip + m, 0, 0)),
            ]
            + [pl.BlockSpec(memory_space=pl.ANY)] * len(whole),
            out_specs=[every_spec, chunk_spec, chunk_spec, chunk_spec],
        ),
        out_shape=[every, chunk, chunk, chunk],
        input_output_aliases={3 + i: i for i in range(len(whole))},
        name="band_sums",
        cost_estimate=pl.CostEstimate(
            flops=2 * slots * cycles * channels * columns,
            bytes_accessed=slots * cycles * columns * 2,
            transcendentals=0,
        ),
    )(me, parts, legendre, *whole)


def final_kernel(mine_ref, near_ref, end_ref, *refs):
    total = mine_ref[...].astype(jnp.float32) + near_ref[...].astype(jnp.float32)
    refs[-1][...] = (total + end_ref[...].astype(jnp.float32)).astype(refs[-1].dtype)


def finish(mine, near, end, first, whole):
    slots, cols, channels = end.shape
    step = 2 if slots % 2 == 0 else 1
    skip = first // step
    every_spec = pl.BlockSpec((step, cols, channels), lambda m: (skip + m, 0, 0))
    chunk_spec = pl.BlockSpec((step, cols, channels), lambda m: (m, 0, 0))
    return pl.pallas_call(
        final_kernel,
        grid=(slots // step,),
        in_specs=[every_spec, chunk_spec, chunk_spec] + [pl.BlockSpec(memory_space=pl.ANY)] * len(whole),
        out_specs=every_spec,
        out_shape=jax.ShapeDtypeStruct(mine.shape, mine.dtype),
        input_output_aliases={3: 0} if whole else {},
        name="finish",
        cost_estimate=pl.CostEstimate(flops=0, bytes_accessed=FINISH_BYTES * slots, transcendentals=0),
    )(mine, near, end, *whole)


def after(value, *earlier):
    return lax.optimization_barrier((value, *earlier))[0]


def add(*values):
    return sum(v.astype(jnp.float32) for v in values).astype(jnp.bfloat16)


def per_device(fourier, cycle_points, wave_table, legendre):
    groups = lax.axis_size("wave")
    me = lax.axis_index("lat")[None]
    sent = make_parts(fourier, cycle_points, wave_table, groups)
    got = lax.all_to_all(sent, "wave", split_axis=0, concat_axis=0, tiled=True)
    _, _, cycles, width, channels = got.shape
    one = [(i, i ^ 1) for i in range(4)]
    two = [(i, i ^ 2) for i in range(4)]
    mine = ()
    crosses, nears, fars = [], [], []
    first = 0
    for size in CHUNKS:
        rows = lax.slice_in_dim(got, first, first + size, axis=3)
        parts = jnp.transpose(rows, (1, 3, 0, 2, 4)).reshape(2, size, groups * cycles, channels)
        whole, near, far, cross = band_sums(me, parts, legendre, first, mine)
        mine = (whole,)
        got = after(got, far)
        crosses.append(lax.ppermute(cross, "lat", one))
        nears.append(near)
        fars.append(far)
        first += size
    (mine,) = mine
    pair = mine
    ends = []
    for i, (far, cross) in enumerate(zip(fars, crosses)):
        pair = add(far, after(cross, pair))
        ends.append(lax.ppermute(pair, "lat", two))
        if LATE:
            nears[i] = after(nears[i], pair)
    out = ()
    first = 0
    for size, near, end in zip(CHUNKS, nears, ends):
        out = (finish(mine, lax.ppermute(near, "lat", one), end, first, out),)
        first += size
    return out[0]


def solution(mesh):
    placed = (P(None, ("lat", "wave"), None, None), P(("lat", "wave")), P(), P("wave", "lat", None))
    return jax.shard_map(
        per_device, mesh=mesh, in_specs=placed, out_specs=P("wave", "lat", None), check_vma=False
    )
```

```python
import functools

import jax
import jax.numpy as jnp
from jax import lax
from jax.experimental import pallas as pl
from jax.experimental.pallas import tpu as pltpu
from jax.sharding import PartitionSpec as P

CHUNKS = (4,4,4,4)
FINISH_BYTES = 8000000
LATE = 1


def parts_kernel(groups, width, points_ref, table_ref, fourier_ref, out_ref):
    cycles = fourier_ref.shape[1]
    channels = fourier_ref.shape[3]
    row = lax.broadcasted_iota(jnp.int32, (width, channels), 0)

    @pl.loop(0, groups, unroll=2)
    def _(q):
        first = pl.multiple_of(table_ref[q * width] // width * width, width)
        rows = pl.ds(first, width)
        for k in range(cycles):
            keep = row < (points_ref[k] + 1) // 2 - first
            north = fourier_ref[0, k, rows, :].astype(jnp.float32)
            south = fourier_ref[1, k, rows, :].astype(jnp.float32)
            out_ref[q, 0, k] = jnp.where(keep, north + south, 0.0).astype(out_ref.dtype)
            out_ref[q, 1, k] = jnp.where(keep, north - south, 0.0).astype(out_ref.dtype)


def make_parts(fourier, cycle_points, wave_table, groups):
    _, cycles, waves, channels = fourier.shape
    width = waves // groups
    return pl.pallas_call(
        functools.partial(parts_kernel, groups, width),
        out_shape=jax.ShapeDtypeStruct((groups, 2, cycles, width, channels), fourier.dtype),
        in_specs=[
            pl.BlockSpec(memory_space=pltpu.SMEM),
            pl.BlockSpec(memory_space=pltpu.SMEM),
            pl.BlockSpec(memory_space=pltpu.VMEM),
        ],
        out_specs=pl.BlockSpec(memory_space=pltpu.VMEM),
        name="make_parts",
    )(cycle_points, wave_table, fourier)


def band_kernel(me_ref, parts_ref, legendre_ref, *refs):
    mine_ref, near_ref, far_ref, cross_ref = refs[-4:]
    me = me_ref[0]
    cols = mine_ref.shape[1]
    for slot in range(mine_ref.shape[0]):
        for flip, ref in ((3, cross_ref), (2, far_ref), (0, mine_ref), (1, near_ref)):
            shard = me ^ flip
            piece = legendre_ref[slot, :, pl.ds(pl.multiple_of(shard * cols, cols), cols)]
            total = lax.dot_general(
                piece, parts_ref[shard // 2, slot], (((0,), (0,)), ((), ())), preferred_element_type=jnp.float32
            )
            ref[slot] = total.astype(ref.dtype)


def band_sums(me, parts, legendre, first, whole):
    _, slots, cycles, channels = parts.shape
    columns = legendre.shape[2]
    cols = columns // 4
    step = 2 if slots % 2 == 0 else 1
    skip = first // step
    every = jax.ShapeDtypeStruct((legendre.shape[0], cols, channels), parts.dtype)
    chunk = jax.ShapeDtypeStruct((slots, cols, channels), parts.dtype)
    every_spec = pl.BlockSpec((step, cols, channels), lambda m, w: (skip + m, 0, 0))
    chunk_spec = pl.BlockSpec((step, cols, channels), lambda m, w: (m, 0, 0))
    return pl.pallas_call(
        band_kernel,
        grid_spec=pltpu.PrefetchScalarGridSpec(
            num_scalar_prefetch=1,
            grid=(slots // step,),
            in_specs=[
                pl.BlockSpec((2, step, cycles, channels), lambda m, w: (0, m, 0, 0)),
                pl.BlockSpec((step, cycles, columns), lambda m, w: (skip + m, 0, 0)),
            ]
            + [pl.BlockSpec(memory_space=pl.ANY)] * len(whole),
            out_specs=[every_spec, chunk_spec, chunk_spec, chunk_spec],
        ),
        out_shape=[every, chunk, chunk, chunk],
        input_output_aliases={3 + i: i for i in range(len(whole))},
        name="band_sums",
        cost_estimate=pl.CostEstimate(
            flops=2 * slots * cycles * channels * columns,
            bytes_accessed=slots * cycles * columns * 2,
            transcendentals=0,
        ),
    )(me, parts, legendre, *whole)


def final_kernel(mine_ref, near_ref, end_ref, *refs):
    total = mine_ref[...].astype(jnp.float32) + near_ref[...].astype(jnp.float32)
    refs[-1][...] = (total + end_ref[...].astype(jnp.float32)).astype(refs[-1].dtype)


def finish(mine, near, end, first, whole):
    slots, cols, channels = end.shape
    step = 2 if slots % 2 == 0 else 1
    skip = first // step
    every_spec = pl.BlockSpec((step, cols, channels), lambda m: (skip + m, 0, 0))
    chunk_spec = pl.BlockSpec((step, cols, channels), lambda m: (m, 0, 0))
    return pl.pallas_call(
        final_kernel,
        grid=(slots // step,),
        in_specs=[every_spec, chunk_spec, chunk_spec] + [pl.BlockSpec(memory_space=pl.ANY)] * len(whole),
        out_specs=every_spec,
        out_shape=jax.ShapeDtypeStruct(mine.shape, mine.dtype),
        input_output_aliases={3: 0} if whole else {},
        name="finish",
        cost_estimate=pl.CostEstimate(flops=0, bytes_accessed=FINISH_BYTES * slots, transcendentals=0),
    )(mine, near, end, *whole)


def after(value, *earlier):
    return lax.optimization_barrier((value, *earlier))[0]


def add(*values):
    return sum(v.astype(jnp.float32) for v in values).astype(jnp.bfloat16)


def per_device(fourier, cycle_points, wave_table, legendre):
    groups = lax.axis_size("wave")
    me = lax.axis_index("lat")[None]
    sent = make_parts(fourier, cycle_points, wave_table, groups)
    got = lax.all_to_all(sent, "wave", split_axis=0, concat_axis=0, tiled=True)
    _, _, cycles, width, channels = got.shape
    one = [(i, i ^ 1) for i in range(4)]
    two = [(i, i ^ 2) for i in range(4)]
    mine = ()
    crosses, nears, fars = [], [], []
    first = 0
    for size in CHUNKS:
        rows = lax.slice_in_dim(got, first, first + size, axis=3)
        parts = jnp.transpose(rows, (1, 3, 0, 2, 4)).reshape(2, size, groups * cycles, channels)
        whole, near, far, cross = band_sums(me, parts, legendre, first, mine)
        mine = (whole,)
        got = after(got, far)
        crosses.append(lax.ppermute(cross, "lat", one))
        nears.append(near)
        fars.append(far)
        first += size
    (mine,) = mine
    pair = mine
    ends, pairs = [], []
    for i, (far, cross) in enumerate(zip(fars, crosses)):
        held = [ends[-2]] if len(ends) >= 2 else []
        pair = add(far, after(cross, pair, *held))
        ends.append(lax.ppermute(pair, "lat", two))
        pairs.append(pair)
    nears = [after(near, pairs[min(i + LATE, len(pairs) - 1)]) for i, near in enumerate(nears)]
    out = ()
    first = 0
    for size, near, end in zip(CHUNKS, nears, ends):
        out = (finish(mine, lax.ppermute(near, "lat", one), end, first, out),)
        first += size
    return out[0]


def solution(mesh):
    placed = (P(None, ("lat", "wave"), None, None), P(("lat", "wave")), P(), P("wave", "lat", None))
    return jax.shard_map(
        per_device, mesh=mesh, in_specs=placed, out_specs=P("wave", "lat", None), check_vma=False
    )
```

```python
import functools

import jax
import jax.numpy as jnp
from jax import lax
from jax.experimental import pallas as pl
from jax.experimental.pallas import tpu as pltpu
from jax.sharding import PartitionSpec as P

CHUNKS = (4,4,4,4)
FINISH_BYTES = 8000000
LATE = 1


def parts_kernel(groups, width, points_ref, table_ref, fourier_ref, out_ref):
    cycles = fourier_ref.shape[1]
    channels = fourier_ref.shape[3]
    row = lax.broadcasted_iota(jnp.int32, (width, channels), 0)

    @pl.loop(0, groups, unroll=2)
    def _(q):
        first = pl.multiple_of(table_ref[q * width] // width * width, width)
        rows = pl.ds(first, width)
        for k in range(cycles):
            keep = row < (points_ref[k] + 1) // 2 - first
            north = fourier_ref[0, k, rows, :].astype(jnp.float32)
            south = fourier_ref[1, k, rows, :].astype(jnp.float32)
            out_ref[q, 0, k] = jnp.where(keep, north + south, 0.0).astype(out_ref.dtype)
            out_ref[q, 1, k] = jnp.where(keep, north - south, 0.0).astype(out_ref.dtype)


def make_parts(fourier, cycle_points, wave_table, groups):
    _, cycles, waves, channels = fourier.shape
    width = waves // groups
    return pl.pallas_call(
        functools.partial(parts_kernel, groups, width),
        out_shape=jax.ShapeDtypeStruct((groups, 2, cycles, width, channels), fourier.dtype),
        in_specs=[
            pl.BlockSpec(memory_space=pltpu.SMEM),
            pl.BlockSpec(memory_space=pltpu.SMEM),
            pl.BlockSpec(memory_space=pltpu.VMEM),
        ],
        out_specs=pl.BlockSpec(memory_space=pltpu.VMEM),
        name="make_parts",
    )(cycle_points, wave_table, fourier)


def band_kernel(me_ref, parts_ref, legendre_ref, *refs):
    mine_ref, near_ref, far_ref, cross_ref = refs[-4:]
    me = me_ref[0]
    cols = mine_ref.shape[1]
    for slot in range(mine_ref.shape[0]):
        for flip, ref in ((3, cross_ref), (2, far_ref), (0, mine_ref), (1, near_ref)):
            shard = me ^ flip
            piece = legendre_ref[slot, :, pl.ds(pl.multiple_of(shard * cols, cols), cols)]
            total = lax.dot_general(
                piece, parts_ref[shard // 2, slot], (((0,), (0,)), ((), ())), preferred_element_type=jnp.float32
            )
            ref[slot] = total.astype(ref.dtype)


def band_sums(me, parts, legendre, first, whole):
    _, slots, cycles, channels = parts.shape
    columns = legendre.shape[2]
    cols = columns // 4
    step = 2 if slots % 2 == 0 else 1
    skip = first // step
    every = jax.ShapeDtypeStruct((legendre.shape[0], cols, channels), parts.dtype)
    chunk = jax.ShapeDtypeStruct((slots, cols, channels), parts.dtype)
    every_spec = pl.BlockSpec((step, cols, channels), lambda m, w: (skip + m, 0, 0))
    chunk_spec = pl.BlockSpec((step, cols, channels), lambda m, w: (m, 0, 0))
    return pl.pallas_call(
        band_kernel,
        grid_spec=pltpu.PrefetchScalarGridSpec(
            num_scalar_prefetch=1,
            grid=(slots // step,),
            in_specs=[
                pl.BlockSpec((2, step, cycles, channels), lambda m, w: (0, m, 0, 0)),
                pl.BlockSpec((step, cycles, columns), lambda m, w: (skip + m, 0, 0)),
            ]
            + [pl.BlockSpec(memory_space=pl.ANY)] * len(whole),
            out_specs=[every_spec, chunk_spec, chunk_spec, chunk_spec],
        ),
        out_shape=[every, chunk, chunk, chunk],
        input_output_aliases={3 + i: i for i in range(len(whole))},
        name="band_sums",
        cost_estimate=pl.CostEstimate(
            flops=2 * slots * cycles * channels * columns,
            bytes_accessed=slots * cycles * columns * 2,
            transcendentals=0,
        ),
    )(me, parts, legendre, *whole)


def final_kernel(mine_ref, near_ref, end_ref, *refs):
    total = mine_ref[...].astype(jnp.float32) + near_ref[...].astype(jnp.float32)
    refs[-1][...] = (total + end_ref[...].astype(jnp.float32)).astype(refs[-1].dtype)


def finish(mine, near, end, first, whole):
    slots, cols, channels = end.shape
    step = 2 if slots % 2 == 0 else 1
    skip = first // step
    every_spec = pl.BlockSpec((step, cols, channels), lambda m: (skip + m, 0, 0))
    chunk_spec = pl.BlockSpec((step, cols, channels), lambda m: (m, 0, 0))
    return pl.pallas_call(
        final_kernel,
        grid=(slots // step,),
        in_specs=[every_spec, chunk_spec, chunk_spec] + [pl.BlockSpec(memory_space=pl.ANY)] * len(whole),
        out_specs=every_spec,
        out_shape=jax.ShapeDtypeStruct(mine.shape, mine.dtype),
        input_output_aliases={3: 0} if whole else {},
        name="finish",
        compiler_params=pltpu.CompilerParams(vmem_limit_bytes=32000000),
        cost_estimate=pl.CostEstimate(flops=0, bytes_accessed=FINISH_BYTES * slots, transcendentals=0),
    )(mine, near, end, *whole)


def after(value, *earlier):
    return lax.optimization_barrier((value, *earlier))[0]


def add(*values):
    return sum(v.astype(jnp.float32) for v in values).astype(jnp.bfloat16)


def per_device(fourier, cycle_points, wave_table, legendre):
    groups = lax.axis_size("wave")
    me = lax.axis_index("lat")[None]
    sent = make_parts(fourier, cycle_points, wave_table, groups)
    got = lax.all_to_all(sent, "wave", split_axis=0, concat_axis=0, tiled=True)
    _, _, cycles, width, channels = got.shape
    one = [(i, i ^ 1) for i in range(4)]
    two = [(i, i ^ 2) for i in range(4)]
    mine = ()
    crosses, nears, fars = [], [], []
    first = 0
    for size in CHUNKS:
        rows = lax.slice_in_dim(got, first, first + size, axis=3)
        parts = jnp.transpose(rows, (1, 3, 0, 2, 4)).reshape(2, size, groups * cycles, channels)
        whole, near, far, cross = band_sums(me, parts, legendre, first, mine)
        mine = (whole,)
        got = after(got, far)
        crosses.append(lax.ppermute(cross, "lat", one))
        nears.append(near)
        fars.append(far)
        first += size
    (mine,) = mine
    pair = mine
    ends, pairs = [], []
    for i, (far, cross) in enumerate(zip(fars, crosses)):
        held = [ends[-2]] if len(ends) >= 2 else []
        pair = add(far, after(cross, pair, *held))
        ends.append(lax.ppermute(pair, "lat", two))
        pairs.append(pair)
    nears = [after(near, pairs[min(i + LATE, len(pairs) - 1)]) for i, near in enumerate(nears)]
    out = ()
    first = 0
    for size, near, end in zip(CHUNKS, nears, ends):
        out = (finish(mine, lax.ppermute(near, "lat", one), end, first, out),)
        first += size
    return out[0]


def solution(mesh):
    placed = (P(None, ("lat", "wave"), None, None), P(("lat", "wave")), P(), P("wave", "lat", None))
    return jax.shard_map(
        per_device, mesh=mesh, in_specs=placed, out_specs=P("wave", "lat", None), check_vma=False
    )
```
